128 devices in a mesh: dp: 16 (over y, x), row: 2 (over core), col: 4 (over z).
Axes of the slice: x: 4, y: 4, z: 4, core: 2. Of those that a mesh axis runs over, the one named last changes fastest.
Arguments:
- hidden: bfloat16 [16384, 14336], P('dp', 'row'), may hold values from -6 to 6
- upstream: bfloat16 [16384, 4096], P('dp', 'col'), may hold values from -0.046875 to 0.046875
- first_codes: int32 [14336, 4096], P(('row', 'dp'), 'col'), may hold values from 0 to 15
- first_scale: float32 [14336, 32], P(('row', 'dp'), 'col'), may hold values from 0.1 to 1
- second_codes: int32 [14336, 4096], P(('row', 'dp'), 'col'), may hold values from 0 to 15
- second_rows: float32 [14336], P(('row', 'dp')), may hold values from 0.004 to 0.04
- second_columns: float32 [4096], P('col'), may hold values from 0.004 to 0.04
Outputs:
- update_step: float32 [14336, 4096], P(('row', 'dp'), 'col')
- first_normed: bfloat16 [14336, 4096], P(('row', 'dp'), 'col')
- first_peak: float32 [14336, 32], P(('row', 'dp'), 'col')
- second_normed: bfloat16 [14336, 4096], P(('row', 'dp'), 'col')
- row_peak: float32 [14336], P(('row', 'dp'))
- column_peak: float32 [4096], P('col')
The draws below stay inside these ranges and needn't reach their ends.
All inputs are finite; a program needn't handle non-finite values. Where the reference program divides by a largest or mean magnitude, that divisor is 1e-20 or more.
Results may differ from the reference program's by a relative error of at most 0.015.
Values may be sent and summed in bfloat16 or wider, within the bound.
No kernel may reach another device: no remote copies, remote signals or barrier semaphores. Data moves between devices by JAX's collectives and lax.ppermute only.
A program may use at most 128 MiB of HBM per device.

```python
import math
import jax
import jax.numpy as jnp
from jax import lax

FFW = 14336
DW = 4096
BLOCK = 128
STEP = 10
TOK_DEV = 1024
TOKENS = 16384
N_DP = 16


def place_ends(entries, key, smallest, high):
    place = [jax.random.randint(jax.random.fold_in(key, axis), (), 0, length) for axis, length in enumerate(entries.shape)]
    longest = entries.shape.index(max(entries.shape))
    next_to = place[:longest] + [(place[longest] + 1) % entries.shape[longest]] + place[longest + 1:]
    return entries.at[tuple(place)].set(smallest).at[tuple(next_to)].set(high)


def level_of(rng, extent, split, smallest, largest):
    def one(position, blocks):
        heights = jax.random.uniform(jax.random.fold_in(jax.random.fold_in(rng, 6), position), (blocks,), jnp.float32, smallest / len(split), largest / len(split))
        return jnp.repeat(jnp.exp(heights), extent[position] // blocks).reshape((-1,) + (1,) * (len(extent) - position - 1))

    level = one(*split[0])
    for cut in split[1:]:
        level = level * one(*cut)
    return level


def centred(stream_key, shape, spread, bound, pieces=(), kind=jnp.bfloat16):
    level = level_of(stream_key, shape, pieces, -0.22, 0.18) if pieces else 1.0
    array = jax.random.normal(stream_key, shape, jnp.float32) * spread * level
    return jnp.minimum(jnp.maximum(array, -bound), bound).astype(kind)


def setup_inputs(seed: int = 0) -> dict:
    splits = jax.random.split(jax.random.key(seed), 8)
    hidden = centred(splits[0], (TOKENS, FFW), 1.0, 6.0, ((0, 16), (1, 2)))
    upstream = centred(splits[1], (TOKENS, DW), TOKENS ** -0.5, 0.046875, ((0, 16), (1, 4)))
    first_codes = place_ends(jax.random.randint(splits[2], (FFW, DW), 0, 16), jax.random.fold_in(splits[2], 1), 0, 15).astype(jnp.int32)
    first_scale = jnp.clip(jnp.exp(math.log(1.0) - 2.3025851 * jax.random.uniform(splits[3], (FFW, DW // BLOCK), jnp.float32) ** level_of(splits[3], (FFW, DW // BLOCK), ((0, 32), (1, 4)), -0.2, 0.2)), 0.1, 1.0)
    second_codes = place_ends(jax.random.randint(splits[4], (FFW, DW), 0, 16), jax.random.fold_in(splits[4], 1), 0, 15).astype(jnp.int32)
    second_rows = jnp.clip(jnp.exp(math.log(0.04) - 2.30258502 * jax.random.uniform(splits[5], (FFW,), jnp.float32) ** level_of(splits[5], (FFW,), ((0, 32),), -0.2, 0.2)), 0.004, 0.04)
    second_columns = jnp.clip(jnp.exp(math.log(0.04) - 2.30258502 * jax.random.uniform(splits[6], (DW,), jnp.float32) ** level_of(splits[6], (DW,), ((0, 4),), -0.2, 0.2)), 0.004, 0.04)
    return {"hidden": hidden, "upstream": upstream, "first_codes": first_codes, "first_scale": first_scale, "second_codes": second_codes, "second_rows": second_rows, "second_columns": second_columns}


def first_table(codes):
    level = codes.astype(jnp.float32)
    upper = level >= 8.0
    expo = jnp.where(upper, level - 8.0, 7.0 - level)
    magnitude = jnp.where(expo > 0.0, jnp.exp2(expo - 7.0), 0.0 * expo)
    return jnp.where(upper, magnitude, -magnitude)

def reference(hidden, upstream, first_codes, first_scale, second_codes, second_rows, second_columns):
    grouped_hidden = hidden.reshape(N_DP, TOK_DEV, FFW)
    grouped_upstream = upstream.reshape(N_DP, TOK_DEV, DW)

    def add_group(total, pair):
        left, right = pair
        partial_value = jnp.dot(left.T, right, preferred_element_type=jnp.float32).astype(jnp.bfloat16)
        return (total + partial_value.astype(jnp.float32), None)
    gradient, _ = lax.scan(add_group, jnp.zeros((FFW, DW), jnp.float32), (grouped_hidden, grouped_upstream))
    block_count = first_scale.shape[1]
    shaped = gradient.reshape(FFW, block_count, -1)
    first_old = first_scale[:, :, None] * first_table(first_codes).reshape(FFW, block_count, -1)
    level_two = (second_codes.astype(jnp.float32) + 1.0) / 16.0
    second_old = jnp.minimum(second_rows[:, None], second_columns[None, :]) * level_two
    second_old = second_old.reshape(FFW, block_count, -1)
    first_new = 0.9 * first_old + 0.1 * shaped
    second_new = 0.999 * second_old + 0.001 * shaped * shaped
    corr_one = 1.0 - 0.9 ** STEP
    corr_two = 1.0 - 0.999 ** STEP
    update_step = first_new / corr_one / (jnp.sqrt(second_new / corr_two) + 1e-08)
    first_peak = lax.optimization_barrier(jnp.max(jnp.abs(first_new), axis=2))
    first_normed = (first_new / (first_peak[:, :, None] + 1e-06)).astype(jnp.bfloat16)
    second_flat = second_new.reshape(FFW, DW)
    row_peak = lax.optimization_barrier(jnp.max(second_flat, axis=1))
    column_peak = lax.optimization_barrier(jnp.max(second_flat, axis=0))
    second_normed = (second_flat / (jnp.minimum(row_peak[:, None], column_peak[None, :]) + 1e-06)).astype(jnp.bfloat16)
    return (update_step.reshape(FFW, DW), first_normed.reshape(FFW, DW), first_peak, second_normed, row_peak, column_peak)
```

```python
import jax
import jax.numpy as jnp
from jax import lax
from jax.experimental import pallas as pl
from jax.experimental.pallas import tpu as pltpu
from jax.sharding import PartitionSpec as P

STEP = 10
F32 = jnp.float32
BF16 = jnp.bfloat16
OWN = 448
HALF = 512
QUART = 256


def first_table(codes):
    level = codes.astype(jnp.float32)
    upper = level >= 8.0
    expo = jnp.where(upper, level - 8.0, 7.0 - level)
    magnitude = jnp.where(expo > 0.0, jnp.exp2(expo - 7.0), 0.0 * expo)
    return jnp.where(upper, magnitude, -magnitude)


def dot(left, right):
    return lax.dot_general(left, right, (((0,), (0,)), ((), ())), preferred_element_type=F32)


def strided_kernel(where, hidden, upstream, low, high, total):
    total[...] = dot(hidden[...], upstream[...])
    start = pl.multiple_of(where[1], 64)
    low[0] = total[pl.ds(start, OWN), :QUART].astype(BF16)
    high[0] = total[pl.ds(start, OWN), QUART:].astype(BF16)


def strided_partial(hidden, upstream, x_to):
    where = jnp.stack([(7 * x_to) >> 1, 64 * (x_to & 1)]).astype(jnp.int32)
    tokens = hidden.shape[0]
    piece = jax.ShapeDtypeStruct((4, OWN, QUART), BF16)
    piece_spec = pl.BlockSpec((1, OWN, QUART), lambda i, s: (i, 0, 0))
    return pl.pallas_call(
        strided_kernel,
        out_shape=(piece, piece),
        grid_spec=pltpu.PrefetchScalarGridSpec(
            num_scalar_prefetch=1,
            grid=(4,),
            in_specs=[
                pl.BlockSpec(
                    (pl.Element(tokens), pl.Element(512)),
                    lambda i, s: (0, pl.multiple_of((14 * i + s[0]) * 128, 128)),
                ),
                pl.BlockSpec((tokens, HALF), lambda i, s: (0, 0)),
            ],
            out_specs=(piece_spec, piece_spec),
            scratch_shapes=[pltpu.VMEM((512, HALF), F32)],
        ),
        cost_estimate=pl.CostEstimate(flops=4 * OWN * HALF * tokens * 2, bytes_accessed=8 << 20, transcendentals=0),
        name="strided",
    )(where, hidden, upstream)


def packed_kernel(where, hidden, upstream, low, high):
    total = dot(hidden[...], upstream[...]).astype(BF16)
    low[...] = total[:, :QUART]
    high[...] = total[:, QUART:]


def packed_partial(hidden, upstream, y_to):
    where = jnp.stack([2 * y_to]).astype(jnp.int32)
    tokens = hidden.shape[0]
    piece = jax.ShapeDtypeStruct((4 * OWN, QUART), BF16)
    piece_spec = pl.BlockSpec((2 * OWN, QUART), lambda i, s: (i, 0))
    low, high = pl.pallas_call(
        packed_kernel,
        out_shape=(piece, piece),
        grid_spec=pltpu.PrefetchScalarGridSpec(
            num_scalar_prefetch=1,
            grid=(2,),
            in_specs=[
                pl.BlockSpec((tokens, 2 * OWN), lambda i, s: (0, s[0] + i)),
                pl.BlockSpec((tokens, HALF), lambda i, s: (0, 1)),
            ],
            out_specs=(piece_spec, piece_spec),
        ),
        cost_estimate=pl.CostEstimate(flops=4 * OWN * HALF * tokens * 2, bytes_accessed=8 << 20, transcendentals=0),
        name="packed",
    )(where, hidden, upstream)
    return low.reshape(4, OWN, QUART), high.reshape(4, OWN, QUART)


def along_x(k):
    return [(4 * y + x, 4 * y + (x + k) % 4) for y in range(4) for x in range(4)]


def along_y(k):
    return [(4 * y + x, 4 * ((y + k) % 4) + x) for y in range(4) for x in range(4)]


def send(value, way, k):
    return lax.ppermute(value, "dp", way(k))


def add(left, right):
    return (left.astype(F32) + right.astype(F32)).astype(BF16)


def first_phase(product, place, way):
    far_low, far_high = product((place + 2) & 3)
    from_left = send(far_low, way, 1)
    from_right = send(far_high, way, -1)
    up_low, up_high = product((place + 1) & 3)
    direct_up = send(up_high, way, 1)
    down_low, down_high = product((place + 3) & 3)
    direct_down = send(down_low, way, -1)
    added_up = send(add(up_low, from_left), way, 1)
    added_down = send(add(down_high, from_right), way, -1)
    own_low, own_high = product(place)
    return (own_low, added_up, direct_down), (own_high, direct_up, added_down)


def second_phase(low, high, place, way):
    def at(arrays, k):
        total = None
        for a in arrays:
            part = lax.dynamic_index_in_dim(a, (place + k) & 3, 0, keepdims=False).astype(F32)
            total = part if total is None else total + part
        return total

    from_left = send(at(low, 2).astype(BF16), way, 1)
    from_right = send(at(high, 2).astype(BF16), way, -1)
    up_high = send(at(high, 1).astype(BF16), way, 1)
    up_low = send((at(low, 1) + from_left.astype(F32)).astype(BF16), way, 1)
    down_low = send(at(low, 3).astype(BF16), way, -1)
    down_high = send((at(high, 3) + from_right.astype(F32)).astype(BF16), way, -1)
    return (
        at(low, 0) + up_low.astype(F32) + down_low.astype(F32),
        at(high, 0) + up_high.astype(F32) + down_high.astype(F32),
    )


def ring_max(value, axis, way):
    parts = [lax.ppermute(value, axis, way(k)) for k in (1, 2, 3)]
    for part in parts:
        value = jnp.maximum(value, part)
    return value


def per_device(
    hidden, upstream, first_codes, first_scale, second_codes, second_rows, second_columns
):
    rows_own = first_codes.shape[0]
    columns = first_codes.shape[1]
    block_count = first_scale.shape[1]
    dp = lax.axis_index("dp")
    x, y = dp & 3, dp >> 2

    a_low, a_high = first_phase(lambda to: strided_partial(hidden, upstream, to), x, along_x)
    b_low, b_high = first_phase(lambda to: packed_partial(hidden, upstream, to), y, along_y)
    a_low, a_high = second_phase(a_low, a_high, y, along_y)
    b_low, b_high = second_phase(b_low, b_high, x, along_x)
    gradient = jnp.concatenate([a_low, a_high, b_low, b_high], axis=1)

    shaped = gradient.reshape(rows_own, block_count, -1)
    first_old = first_scale[:, :, None] * first_table(first_codes).reshape(
        rows_own, block_count, -1
    )
    level_two = (second_codes.astype(jnp.float32) + 1.0) / 16.0
    second_old = (jnp.minimum(second_rows[:, None], second_columns[None, :]) * level_two).reshape(
        rows_own, block_count, -1
    )
    first_new = 0.9 * first_old + 0.1 * shaped
    second_new = 0.999 * second_old + 0.001 * shaped * shaped
    corr_one = 1.0 - 0.9**STEP
    corr_two = 1.0 - 0.999**STEP
    update_step = first_new / corr_one / (jnp.sqrt(second_new / corr_two) + 1e-08)
    first_peak = jnp.max(jnp.abs(first_new), axis=2)
    first_normed = (first_new / (first_peak[:, :, None] + 1e-06)).astype(jnp.bfloat16)
    second_flat = second_new.reshape(rows_own, columns)
    row_part = jnp.max(second_flat, axis=1)
    column_part = jnp.max(second_flat, axis=0)
    row_peak = ring_max(row_part, "col", lambda k: [(z, (z + k) % 4) for z in range(4)])
    column_peak = jnp.maximum(column_part, lax.ppermute(column_part, "row", [(0, 1), (1, 0)]))
    column_peak = ring_max(column_peak, "dp", along_x)
    column_peak = ring_max(column_peak, "dp", along_y)
    second_normed = (
        second_flat / (jnp.minimum(row_peak[:, None], column_peak[None, :]) + 1e-06)
    ).astype(jnp.bfloat16)
    return (
        update_step.reshape(rows_own, columns),
        first_normed.reshape(rows_own, columns),
        first_peak,
        second_normed,
        row_peak,
        column_peak,
    )


def solution(mesh):
    placed = (
        P("dp", "row"),
        P("dp", "col"),
        P(("row", "dp"), "col"),
        P(("row", "dp"), "col"),
        P(("row", "dp"), "col"),
        P(("row", "dp")),
        P("col"),
    )
    return jax.shard_map(
        per_device,
        mesh=mesh,
        in_specs=placed,
        out_specs=(
            P(("row", "dp"), "col"),
            P(("row", "dp"), "col"),
            P(("row", "dp"), "col"),
            P(("row", "dp"), "col"),
            P(("row", "dp")),
            P("col"),
        ),
        check_vma=False,
    )
```

```python
import functools

import jax
import jax.numpy as jnp
from jax import lax
from jax.experimental import pallas as pl
from jax.experimental.pallas import tpu as pltpu
from jax.sharding import PartitionSpec as P


STEP = 10
F32 = jnp.float32
BF16 = jnp.bfloat16
OWN = 448
HALF = 512
SPAN = 512
LANES = 128
CORR_ONE = 1.0 - 0.9**STEP
CORR_TWO = 1.0 - 0.999**STEP
ANY = pl.BlockSpec(memory_space=pl.ANY)


GRANT = pltpu.CompilerParams(vmem_limit_bytes=58 << 20)


def dot(left, right):
    return lax.dot_general(left, right, (((0,), (0,)), ((), ())), preferred_element_type=F32)


def product_kernel(base, added, where, hidden, upstream, *refs):
    received = refs[:2] if added else ()
    outs = refs[len(received) : len(received) + 2]
    held, features, got, made, total, sems = refs[len(received) + 2 :]
    loads = [
        pltpu.make_async_copy(
            hidden.at[:, pl.ds(pl.multiple_of(where[base + i] * LANES, LANES), SPAN)],
            held.at[i],
            sems.at[i],
        )
        for i in range(4)
    ]
    feature_copy = pltpu.make_async_copy(upstream, features, sems.at[4])
    got_copies = [
        pltpu.make_async_copy(received[d], got.at[d], sems.at[5 + d]) for d in range(len(received))
    ]
    feature_copy.start()
    for copy in loads:
        copy.start()
    for copy in got_copies:
        copy.start()
    feature_copy.wait()
    stores = []
    for i in range(4):
        loads[i].wait()
        total[i % 2] = dot(held[i], features[...])
        start = pl.multiple_of(where[16 + base + i], 64)
        if i == 0:
            for copy in got_copies:
                copy.wait()
        for d in range(2):
            value = total[i % 2, pl.ds(start, OWN), d * HALF : (d + 1) * HALF]
            if added:
                value = value + got[d, i].astype(F32)
            made[d, i] = value.astype(BF16)
            copy = pltpu.make_async_copy(made.at[d, i], outs[d].at[i], sems.at[7 + 2 * i + d])
            copy.start()
            stores.append(copy)
    for copy in stores:
        copy.wait()


def product(hidden, upstream, where, base, received=()):
    tokens, width = upstream.shape
    piece = jax.ShapeDtypeStruct((4, OWN, HALF), BF16)
    return pl.pallas_call(
        functools.partial(product_kernel, base, bool(received)),
        out_shape=(piece, piece),
        grid_spec=pltpu.PrefetchScalarGridSpec(
            num_scalar_prefetch=1,
            grid=(1,),
            in_specs=[ANY] * (2 + len(received)),
            out_specs=(ANY, ANY),
            scratch_shapes=[
                pltpu.VMEM((4, tokens, SPAN), BF16),
                pltpu.VMEM((tokens, width), BF16),
                pltpu.VMEM((2, 4, OWN, HALF) if received else (2, 1, 16, 128), BF16),
                pltpu.VMEM((2, 4, OWN, HALF), BF16),
                pltpu.VMEM((2, SPAN, width), F32),
                pltpu.SemaphoreType.DMA((15,)),
            ],
        ),
        cost_estimate=pl.CostEstimate(
            flops=8 * OWN * tokens * width, bytes_accessed=10 << 20, transcendentals=0
        ),
        compiler_params=GRANT,
    )(where, hidden, upstream, *received)


def ring(first_core, k):
    pairs = []
    for y in range(4):
        for x in range(4):
            for core in range(2):
                along_x = core == first_core
                to = 4 * y + (x + k) % 4 if along_x else 4 * ((y + k) % 4) + x
                pairs.append((2 * (4 * y + x) + core, 2 * to + core))
    return pairs


def near(k):
    return ring(0, k)


def other(k):
    return ring(1, k)


def send(value, pairs):
    return lax.ppermute(value, ("dp", "row"), pairs)


def sum_kernel(kept, got, far, up, down, held, made, sems):
    outs = (far, up, down)
    loads = [
        [
            pltpu.make_async_copy(a.at[k], held.at[k, n], sems.at[2 * k + n])
            for n, a in enumerate((kept, got))
        ]
        for k in range(3)
    ]
    for group in loads:
        for copy in group:
            copy.start()
    stores = []
    for k in range(3):
        for copy in loads[k]:
            copy.wait()
        made[k] = (held[k, 0].astype(F32) + held[k, 1].astype(F32)).astype(BF16)
        copy = pltpu.make_async_copy(made.at[k], outs[k], sems.at[6 + k])
        copy.start()
        stores.append(copy)
    for copy in stores:
        copy.wait()


def last(kept, got):
    message = jax.ShapeDtypeStruct((OWN, HALF), BF16)
    far, up, down = pl.pallas_call(
        sum_kernel,
        out_shape=(message,) * 3,
        in_specs=[ANY] * 2,
        out_specs=(ANY,) * 3,
        scratch_shapes=[
            pltpu.VMEM((3, 2, OWN, HALF), BF16),
            pltpu.VMEM((3, OWN, HALF), BF16),
            pltpu.SemaphoreType.DMA((9,)),
        ],
        cost_estimate=pl.CostEstimate(
            flops=3 * OWN * HALF, bytes_accessed=4 << 20, transcendentals=0
        ),
        compiler_params=GRANT,
    )(kept, got)
    return (send(far, other(2)), send(up, other(1)), send(down, other(-1)))


def add(left, right):
    return (left.astype(F32) + right.astype(F32)).astype(BF16)


def reduced(hidden, upstream, owner):
    owners = jnp.stack([owner(p, q) for p in (2, 1, 3, 0) for q in (2, 1, 3, 0)])
    where = jnp.concatenate([(7 * owners) >> 1, 64 * (owners & 1)]).astype(jnp.int32)
    far_low, far_high = product(hidden, upstream, where, 0)
    from_low = send(far_low, near(1))
    from_high = send(far_high, near(-1))
    up_low, up_high = product(hidden, upstream, where, 4)
    direct_high = send(up_high, near(1))
    down_low, down_high = product(hidden, upstream, where, 8)
    direct_low = send(down_low, near(-1))
    added_low = send(add(up_low[:3], from_low[:3]), near(1))
    added_high = send(add(down_high[:3], from_high[:3]), near(-1))
    added_low_own = send(add(up_low[3], from_low[3]), near(1))
    added_high_own = send(add(down_high[3], from_high[3]), near(-1))
    own_low, own_high = product(hidden, upstream, where, 12, (direct_low, direct_high))
    return (
        (own_low, added_low_own, *last(own_low, added_low)),
        (own_high, added_high_own, *last(own_high, added_high)),
    )


TALL = 112
CHUNKS = OWN // TALL


def second_kernel(half, own, added, far, up, down, codes, rows, columns, *refs):
    before, refs = (refs[:2], refs[2:]) if half else ((), refs)
    gradient, second, row_out, column_out = refs[:4]
    parts, code, row, column, made, wide, sems = refs[4:]
    here = pl.ds(half * HALF, HALF)
    small = [
        pltpu.make_async_copy(rows, row, sems.at[0]),
        pltpu.make_async_copy(columns.at[:, here], column, sems.at[1]),
    ]
    loads = []
    for i in range(CHUNKS):
        at = pl.ds(i * TALL, TALL)
        sources = [own.at[3, at], added.at[at], far.at[at], up.at[at], down.at[at]]
        group = [
            pltpu.make_async_copy(a, parts.at[n, at], sems.at[2 + 6 * i + n])
            for n, a in enumerate(sources)
        ]
        group.append(
            pltpu.make_async_copy(codes.at[at, here], code.at[at], sems.at[2 + 6 * i + 5])
        )
        loads.append(group)
    for copy in small:
        copy.start()
    for group in loads:
        for copy in group:
            copy.start()
    for copy in small:
        copy.wait()
    peak = None
    stores = []
    for i in range(CHUNKS):
        at = pl.ds(i * TALL, TALL)
        for copy in loads[i]:
            copy.wait()
        total = parts[0, at, :].astype(F32)
        for n in range(1, 5):
            total = total + parts[n, at, :].astype(F32)
        level = (code[at, :].astype(F32) + 1.0) / 16.0
        old = jnp.minimum(row[at, :], column[...]) * level
        new = 0.999 * old + 0.001 * total * total
        made[0, at, :] = total
        made[1, at, :] = new
        for n, out in enumerate((gradient, second)):
            copy = pltpu.make_async_copy(
                made.at[n, at], out.at[at], sems.at[2 + 6 * CHUNKS + 2 * i + n]
            )
            copy.start()
            stores.append(copy)
        top = jnp.max(new, axis=0, keepdims=True)
        peak = top if peak is None else jnp.maximum(peak, top)
        widest = new[:, :LANES]
        for b in range(1, HALF // LANES):
            widest = jnp.maximum(widest, new[:, b * LANES : (b + 1) * LANES])
        wide[at, :] = widest
    row_top = jnp.max(wide[...].T, axis=0, keepdims=True)
    if half:
        row_out[...] = jnp.maximum(row_top, before[0][...])
        column_out[:, :HALF] = before[1][...]
        column_out[:, HALF:] = peak
    else:
        row_out[...] = row_top
        column_out[...] = peak
    for copy in stores:
        copy.wait()


def second_moment(half, parts, codes, rows, columns, before=()):
    vmem = pl.BlockSpec(memory_space=pltpu.MemorySpace.VMEM)
    reach = HALF * (1 + half)
    return pl.pallas_call(
        functools.partial(second_kernel, half),
        out_shape=(
            jax.ShapeDtypeStruct((OWN, HALF), F32),
            jax.ShapeDtypeStruct((OWN, HALF), F32),
            jax.ShapeDtypeStruct((1, OWN), F32),
            jax.ShapeDtypeStruct((1, reach), F32),
        ),
        in_specs=[ANY] * 8 + [vmem] * len(before),
        out_specs=(ANY, ANY, vmem, vmem),
        scratch_shapes=[
            pltpu.VMEM((5, OWN, HALF), BF16),
            pltpu.VMEM((OWN, HALF), jnp.int32),
            pltpu.VMEM((OWN, 1), F32),
            pltpu.VMEM((1, HALF), F32),
            pltpu.VMEM((2, OWN, HALF), F32),
            pltpu.VMEM((OWN, LANES), F32),
            pltpu.SemaphoreType.DMA((2 + 8 * CHUNKS,)),
        ],
        cost_estimate=pl.CostEstimate(
            flops=20 * OWN * HALF, bytes_accessed=5 << 20, transcendentals=0
        ),
        compiler_params=GRANT,
    )(*parts, codes, rows, columns, *before)


def first_kernel(half, gradient, second, codes, scale, *refs):
    update, normed, peaks = refs[-3:]
    blocks = HALF // LANES
    for b in range(blocks):
        here = slice(b * LANES, (b + 1) * LANES)
        block = half * blocks + b
        code = codes[:, here]
        upper = code >= 8
        expo = jnp.where(upper, code - 8, 7 - code)
        magnitude = jnp.where(expo > 0, lax.shift_left(jnp.ones_like(expo), expo), 0)
        table = jnp.where(upper, magnitude, -magnitude).astype(F32) * (1.0 / 128.0)
        new = 0.9 * (scale[:, block : block + 1] * table) + 0.1 * gradient[:, here]
        update[:, here] = new / CORR_ONE / (jnp.sqrt(second[:, here] / CORR_TWO) + 1e-08)
        peak = jnp.max(jnp.abs(new), axis=1, keepdims=True)
        normed[:, here] = (new / (peak + 1e-06)).astype(BF16)
        peaks[:, block : block + 1] = peak
    for b in range(blocks):
        kept = (1 - half) * blocks + b
        if half:
            peaks[:, kept : kept + 1] = refs[0][:, kept : kept + 1]
        else:
            peaks[:, kept : kept + 1] = jnp.zeros((peaks.shape[0], 1), F32)


def first_moment(half, gradient, second, codes, scale, before=()):
    rows, width = codes.shape
    blocks = scale.shape[1]
    half_spec = pl.BlockSpec((TALL, HALF), lambda i: (i, 0))
    there_spec = pl.BlockSpec((TALL, HALF), lambda i: (i, half))
    peak_spec = pl.BlockSpec((TALL, blocks), lambda i: (i, 0))
    return pl.pallas_call(
        functools.partial(first_kernel, half),
        out_shape=(
            jax.ShapeDtypeStruct((rows, width), F32),
            jax.ShapeDtypeStruct((rows, width), BF16),
            jax.ShapeDtypeStruct((rows, blocks), F32),
        ),
        grid=(CHUNKS,),
        in_specs=[half_spec, half_spec, there_spec, peak_spec]
        + ([peak_spec, ANY, ANY] if half else []),
        out_specs=(there_spec, there_spec, peak_spec),
        input_output_aliases={5: 0, 6: 1} if half else {},
        cost_estimate=pl.CostEstimate(
            flops=40 * rows * HALF, bytes_accessed=5 << 20, transcendentals=rows * HALF
        ),
        compiler_params=GRANT,
    )(gradient, second, codes, scale, *before)


def norm_kernel(low, high, row_peak, column_peak, normed):
    rows = low.shape[0]
    row = jnp.broadcast_to(row_peak[...], (LANES, rows)).T
    for n, second in enumerate((low, high)):
        for b in range(HALF // LANES):
            here = slice(b * LANES, (b + 1) * LANES)
            there = slice(n * HALF + b * LANES, n * HALF + (b + 1) * LANES)
            peak = jnp.minimum(row, column_peak[:, there]) + 1e-06
            normed[:, there] = (second[:, here] / peak).astype(BF16)


def norm_second(low, high, row_peak, column_peak):
    return pl.pallas_call(
        norm_kernel,
        out_shape=jax.ShapeDtypeStruct((OWN, 2 * HALF), BF16),
        compiler_params=GRANT,
        name="norm",
    )(low, high, row_peak, column_peak)


def ring_max(value, axis, way):
    parts = []
    for k in (1, 2, 3):
        parts.append(lax.ppermute(value, axis, way(k)))
    for part in parts:
        value = jnp.maximum(value, part)
    return value


def per_device(
    hidden, upstream, first_codes, first_scale, second_codes, second_rows, second_columns
):
    dp, core = lax.axis_index("dp"), lax.axis_index("row")
    x, y = dp & 3, dp >> 2

    def owner(p, q):
        along_x, along_y = jnp.where(core == 0, p, q), jnp.where(core == 0, q, p)
        return 4 * ((y + along_y) & 3) + ((x + along_x) & 3)

    low, high = reduced(hidden, upstream, owner)
    rows, columns = second_rows[:, None], second_columns[None, :]
    gradient_low, second_low, row_low, column_low = second_moment(
        0, low, second_codes, rows, columns
    )
    done = first_moment(0, gradient_low, second_low, first_codes, first_scale)
    gradient_high, second_high, row_peak, column_peak = second_moment(
        1, high, second_codes, rows, columns, (row_low, column_low)
    )
    both = ("dp", "row")
    partner = lax.ppermute(column_peak, "row", [(0, 1), (1, 0)])
    for k in (1, 2):
        beside = lax.ppermute(row_peak, "col", [(z, z ^ k) for z in range(4)])
        row_peak = jnp.maximum(row_peak, beside)
    column_peak = ring_max(jnp.maximum(column_peak, partner), both, near)
    column_peak = ring_max(column_peak, both, other)
    update_step, first_normed, first_peak = first_moment(
        1, gradient_high, second_high, first_codes, first_scale, (done[2], done[0], done[1])
    )
    second_normed = norm_second(second_low, second_high, row_peak, column_peak)
    return (
        update_step,
        first_normed,
        first_peak,
        second_normed,
        row_peak.reshape(-1),
        column_peak.reshape(-1),
    )


def solution(mesh):
    placed = (
        P("dp", "row"),
        P("dp", "col"),
        P(("row", "dp"), "col"),
        P(("row", "dp"), "col"),
        P(("row", "dp"), "col"),
        P(("row", "dp")),
        P("col"),
    )
    return jax.shard_map(
        per_device,
        mesh=mesh,
        in_specs=placed,
        out_specs=(
            P(("row", "dp"), "col"),
            P(("row", "dp"), "col"),
            P(("row", "dp"), "col"),
            P(("row", "dp"), "col"),
            P(("row", "dp")),
            P("col"),
        ),
        check_vma=False,
    )
```

```python
import functools

import jax
import jax.numpy as jnp
from jax import lax
from jax.experimental import pallas as pl
from jax.experimental.pallas import tpu as pltpu
from jax.sharding import PartitionSpec as P


STEP = 10
F32 = jnp.float32
BF16 = jnp.bfloat16
OWN = 448
HALF = 512
SPAN = 512
LANES = 128
CORR_ONE = 1.0 - 0.9**STEP
CORR_TWO = 1.0 - 0.999**STEP
ANY = pl.BlockSpec(memory_space=pl.ANY)


SMALL = pltpu.CompilerParams(vmem_limit_bytes=16 << 20)
GRANT = pltpu.CompilerParams(vmem_limit_bytes=58 << 20)


def in_hbm(a):
    return pltpu.with_memory_space_constraint(a, pltpu.MemorySpace.HBM)


def dot(left, right):
    return lax.dot_general(left, right, (((0,), (0,)), ((), ())), preferred_element_type=F32)


def product_kernel(base, added, where, hidden, upstream, *refs):
    received = refs[:2] if added else ()
    outs = refs[len(received) : len(received) + 2]
    held, features, got, made, total, sems = refs[len(received) + 2 :]
    loads = [
        pltpu.make_async_copy(
            hidden.at[:, pl.ds(pl.multiple_of(where[base + i] * LANES, LANES), SPAN)],
            held.at[i],
            sems.at[i],
        )
        for i in range(4)
    ]
    feature_copy = pltpu.make_async_copy(upstream, features, sems.at[4])
    got_copies = [
        pltpu.make_async_copy(received[d], got.at[d], sems.at[5 + d]) for d in range(len(received))
    ]
    feature_copy.start()
    for copy in loads:
        copy.start()
    for copy in got_copies:
        copy.start()
    feature_copy.wait()
    stores = []
    for i in range(4):
        loads[i].wait()
        total[i % 2] = dot(held[i], features[...])
        start = pl.multiple_of(where[16 + base + i], 64)
        if i == 0:
            for copy in got_copies:
                copy.wait()
        for d in range(2):
            value = total[i % 2, pl.ds(start, OWN), d * HALF : (d + 1) * HALF]
            if added:
                value = value + got[d, i].astype(F32)
            made[d, i] = value.astype(BF16)
            copy = pltpu.make_async_copy(made.at[d, i], outs[d].at[i], sems.at[7 + 2 * i + d])
            copy.start()
            stores.append(copy)
    for copy in stores:
        copy.wait()


def product(hidden, upstream, where, base, received=()):
    tokens, width = upstream.shape
    piece = jax.ShapeDtypeStruct((4, OWN, HALF), BF16)
    return pl.pallas_call(
        functools.partial(product_kernel, base, bool(received)),
        out_shape=(piece, piece),
        grid_spec=pltpu.PrefetchScalarGridSpec(
            num_scalar_prefetch=1,
            grid=(1,),
            in_specs=[ANY] * (2 + len(received)),
            out_specs=(ANY, ANY),
            scratch_shapes=[
                pltpu.VMEM((4, tokens, SPAN), BF16),
                pltpu.VMEM((tokens, width), BF16),
                pltpu.VMEM((2, 4, OWN, HALF) if received else (2, 1, 16, 128), BF16),
                pltpu.VMEM((2, 4, OWN, HALF), BF16),
                pltpu.VMEM((2, SPAN, width), F32),
                pltpu.SemaphoreType.DMA((15,)),
            ],
        ),
        cost_estimate=pl.CostEstimate(
            flops=8 * OWN * tokens * width, bytes_accessed=10 << 20, transcendentals=0
        ),
        compiler_params=GRANT,
    )(where, hidden, upstream, *received)


def ring(first_core, k):
    pairs = []
    for y in range(4):
        for x in range(4):
            for core in range(2):
                along_x = core == first_core
                to = 4 * y + (x + k) % 4 if along_x else 4 * ((y + k) % 4) + x
                pairs.append((2 * (4 * y + x) + core, 2 * to + core))
    return pairs


def near(k):
    return ring(0, k)


def other(k):
    return ring(1, k)


def send(value, pairs):
    return lax.ppermute(value, ("dp", "row"), pairs)


def sum_kernel(kept, got, far, up, down, held, made, sems):
    outs = (far, up, down)
    loads = [
        [
            pltpu.make_async_copy(a.at[k], held.at[k, n], sems.at[2 * k + n])
            for n, a in enumerate((kept, got))
        ]
        for k in range(3)
    ]
    for group in loads:
        for copy in group:
            copy.start()
    stores = []
    for k in range(3):
        for copy in loads[k]:
            copy.wait()
        made[k] = (held[k, 0].astype(F32) + held[k, 1].astype(F32)).astype(BF16)
        copy = pltpu.make_async_copy(made.at[k], outs[k], sems.at[6 + k])
        copy.start()
        stores.append(copy)
    for copy in stores:
        copy.wait()


def last(kept, got):
    message = jax.ShapeDtypeStruct((OWN, HALF), BF16)
    far, up, down = pl.pallas_call(
        sum_kernel,
        out_shape=(message,) * 3,
        in_specs=[ANY] * 2,
        out_specs=(ANY,) * 3,
        scratch_shapes=[
            pltpu.VMEM((3, 2, OWN, HALF), BF16),
            pltpu.VMEM((3, OWN, HALF), BF16),
            pltpu.SemaphoreType.DMA((9,)),
        ],
        cost_estimate=pl.CostEstimate(
            flops=3 * OWN * HALF, bytes_accessed=4 << 20, transcendentals=0
        ),
        compiler_params=SMALL,
    )(kept, got)
    return (send(far, other(2)), send(up, other(1)), send(down, other(-1)))


def add(left, right):
    return (left.astype(F32) + right.astype(F32)).astype(BF16)


def reduced(hidden, upstream, owner):
    owners = jnp.stack([owner(p, q) for p in (2, 1, 3, 0) for q in (2, 1, 3, 0)])
    where = jnp.concatenate([(7 * owners) >> 1, 64 * (owners & 1)]).astype(jnp.int32)
    far_low, far_high = product(hidden, upstream, where, 0)
    from_low = send(far_low, near(1))
    from_high = send(far_high, near(-1))
    up_low, up_high = product(hidden, upstream, where, 4)
    direct_high = send(up_high, near(1))
    down_low, down_high = product(hidden, upstream, where, 8)
    direct_low = send(down_low, near(-1))
    added_low = send(add(up_low[:3], from_low[:3]), near(1))
    added_high = send(add(down_high[:3], from_high[:3]), near(-1))
    added_low_own = send(add(up_low[3], from_low[3]), near(1))
    added_high_own = send(add(down_high[3], from_high[3]), near(-1))
    own_low, own_high = product(hidden, upstream, where, 12, (direct_low, direct_high))
    kept_low, kept_high = in_hbm(own_low), in_hbm(own_high)
    return (
        (own_low[3].astype(F32) + added_low_own.astype(F32), *last(kept_low, added_low)),
        (own_high[3].astype(F32) + added_high_own.astype(F32), *last(kept_high, added_high)),
    )


TALL = 112
CHUNKS = OWN // TALL


def second_kernel(half, own, far, up, down, codes, rows, columns, *refs):
    before, refs = (refs[:2], refs[2:]) if half else ((), refs)
    gradient, second, row_out, column_out, wide = refs
    i = pl.program_id(0)
    total = own[...]
    for ref in (far, up, down):
        total = total + ref[...].astype(F32)
    level = (codes[...].astype(F32) + 1.0) / 16.0
    old = jnp.minimum(rows[...], columns[...]) * level
    new = 0.999 * old + 0.001 * total * total
    gradient[...] = total
    second[...] = new
    peak = jnp.max(new, axis=0, keepdims=True)
    here = slice(half * HALF, (half + 1) * HALF)

    @pl.when(i == 0)
    def _():
        column_out[:, here] = peak
        if half:
            column_out[:, :HALF] = before[1][...]

    @pl.when(i > 0)
    def _():
        column_out[:, here] = jnp.maximum(column_out[:, here], peak)

    widest = new[:, :LANES]
    for b in range(1, HALF // LANES):
        widest = jnp.maximum(widest, new[:, b * LANES : (b + 1) * LANES])
    wide[pl.ds(pl.multiple_of(i * TALL, TALL), TALL), :] = widest

    @pl.when(i == pl.num_programs(0) - 1)
    def _():
        row_top = jnp.max(wide[...].T, axis=0, keepdims=True)
        row_out[...] = jnp.maximum(row_top, before[0][...]) if half else row_top


def second_moment(half, parts, codes, rows, columns, before=()):
    reach = HALF * (1 + half)
    half_spec = pl.BlockSpec((TALL, HALF), lambda i: (i, 0))

    def whole(width):
        return pl.BlockSpec((1, width), lambda i: (0, 0))

    return pl.pallas_call(
        functools.partial(second_kernel, half),
        out_shape=(
            jax.ShapeDtypeStruct((OWN, HALF), F32),
            jax.ShapeDtypeStruct((OWN, HALF), F32),
            jax.ShapeDtypeStruct((1, OWN), F32),
            jax.ShapeDtypeStruct((1, reach), F32),
        ),
        grid=(CHUNKS,),
        in_specs=[half_spec] * 4
        + [
            pl.BlockSpec((TALL, HALF), lambda i: (i, half)),
            pl.BlockSpec((TALL, 1), lambda i: (i, 0)),
            pl.BlockSpec((1, HALF), lambda i: (0, half)),
        ]
        + ([whole(OWN), whole(HALF)] if half else []),
        out_specs=(half_spec, half_spec, whole(OWN), whole(reach)),
        scratch_shapes=[pltpu.VMEM((OWN, LANES), F32)],
        cost_estimate=pl.CostEstimate(
            flops=20 * OWN * HALF, bytes_accessed=5 << 20, transcendentals=0
        ),
        compiler_params=SMALL,
    )(*parts, codes, rows, columns, *before)


def first_kernel(half, gradient, second, codes, scale, *refs):
    update, normed, peaks, tops = refs[-4:]
    blocks = HALF // LANES
    for b in range(blocks):
        here = slice(b * LANES, (b + 1) * LANES)
        block = half * blocks + b
        code = codes[:, here]
        upper = code >= 8
        expo = jnp.where(upper, code - 8, 7 - code)
        magnitude = jnp.where(expo > 0, lax.shift_left(jnp.ones_like(expo), expo), 0)
        table = jnp.where(upper, magnitude, -magnitude).astype(F32) * (1.0 / 128.0)
        new = 0.9 * (scale[:, block : block + 1] * table) + 0.1 * gradient[:, here]
        update[:, here] = new / CORR_ONE / (jnp.sqrt(second[:, here] / CORR_TWO) + 1e-08)
        peak = jnp.max(jnp.abs(new), axis=1, keepdims=True)
        normed[:, here] = (new / (peak + 1e-06)).astype(BF16)
        at = pl.ds(pl.multiple_of(pl.program_id(0) * TALL, TALL), TALL)
        tops[at, b : b + 1] = peak

    @pl.when(pl.program_id(0) == pl.num_programs(0) - 1)
    def _():
        mine = tops[...].T[:blocks]
        rest = refs[0][:blocks, :] if half else mine
        peaks[...] = jnp.concatenate([rest, mine] if half else [mine, rest], axis=0)


def first_moment(half, gradient, second, codes, scale, before=()):
    rows, width = codes.shape
    blocks = scale.shape[1]
    half_spec = pl.BlockSpec((TALL, HALF), lambda i: (i, 0))
    there_spec = pl.BlockSpec((TALL, HALF), lambda i: (i, half))
    scale_spec = pl.BlockSpec((TALL, blocks), lambda i: (i, 0))
    peak_spec = pl.BlockSpec((blocks, rows), lambda i: (0, 0))
    return pl.pallas_call(
        functools.partial(first_kernel, half),
        out_shape=(
            jax.ShapeDtypeStruct((rows, width), F32),
            jax.ShapeDtypeStruct((rows, width), BF16),
            jax.ShapeDtypeStruct((blocks, rows), F32),
        ),
        grid=(CHUNKS,),
        in_specs=[half_spec, half_spec, there_spec, scale_spec]
        + ([peak_spec, ANY, ANY] if half else []),
        out_specs=(there_spec, there_spec, peak_spec),
        scratch_shapes=[pltpu.VMEM((rows, LANES), F32)],
        input_output_aliases={5: 0, 6: 1} if half else {},
        cost_estimate=pl.CostEstimate(
            flops=40 * rows * HALF, bytes_accessed=5 << 20, transcendentals=rows * HALF
        ),
        compiler_params=SMALL,
    )(gradient, second, codes, scale, *before)


def norm_kernel(low, high, row_peak, column_peak, normed):
    rows = low.shape[0]
    row = jnp.broadcast_to(row_peak[...], (LANES, rows)).T
    for n, second in enumerate((low, high)):
        for b in range(HALF // LANES):
            here = slice(b * LANES, (b + 1) * LANES)
            there = slice(n * HALF + b * LANES, n * HALF + (b + 1) * LANES)
            peak = jnp.minimum(row, column_peak[:, there]) + 1e-06
            normed[:, there] = (second[:, here] / peak).astype(BF16)


def norm_second(low, high, row_peak, column_peak):
    return pl.pallas_call(
        norm_kernel,
        out_shape=jax.ShapeDtypeStruct((OWN, 2 * HALF), BF16),
        compiler_params=SMALL,
        name="norm",
    )(low, high, row_peak, column_peak)


def ring_max(value, axis, way):
    parts = []
    for k in (1, 2, 3):
        parts.append(lax.ppermute(value, axis, way(k)))
    for part in parts:
        value = jnp.maximum(value, part)
    return value


def per_device(
    hidden, upstream, first_codes, first_scale, second_codes, second_rows, second_columns
):
    dp, core = lax.axis_index("dp"), lax.axis_index("row")
    x, y = dp & 3, dp >> 2

    def owner(p, q):
        along_x, along_y = jnp.where(core == 0, p, q), jnp.where(core == 0, q, p)
        return 4 * ((y + along_y) & 3) + ((x + along_x) & 3)

    low, high = reduced(hidden, upstream, owner)
    rows, columns = second_rows[:, None], second_columns[None, :]
    gradient_low, second_low, row_low, column_low = second_moment(
        0, low, second_codes, rows, columns
    )
    done = first_moment(0, gradient_low, second_low, first_codes, first_scale)
    gradient_high, second_high, row_peak, column_peak = second_moment(
        1, high, second_codes, rows, columns, (row_low, column_low)
    )
    both = ("dp", "row")
    partner = lax.ppermute(column_peak, "row", [(0, 1), (1, 0)])
    for k in (1, 3):
        beside = lax.ppermute(row_peak, "col", [(z, z ^ k) for z in range(4)])
        row_peak = jnp.maximum(row_peak, beside)
    column_peak = ring_max(jnp.maximum(column_peak, partner), both, near)
    column_peak = ring_max(column_peak, both, other)
    update_step, first_normed, first_peak = first_moment(
        1, gradient_high, second_high, first_codes, first_scale, (done[2], done[0], done[1])
    )
    second_normed = norm_second(second_low, second_high, row_peak, column_peak)
    return (
        update_step,
        first_normed,
        first_peak.T,
        second_normed,
        row_peak.reshape(-1),
        column_peak.reshape(-1),
    )


def solution(mesh):
    placed = (
        P("dp", "row"),
        P("dp", "col"),
        P(("row", "dp"), "col"),
        P(("row", "dp"), "col"),
        P(("row", "dp"), "col"),
        P(("row", "dp")),
        P("col"),
    )
    return jax.shard_map(
        per_device,
        mesh=mesh,
        in_specs=placed,
        out_specs=(
            P(("row", "dp"), "col"),
            P(("row", "dp"), "col"),
            P(("row", "dp"), "col"),
            P(("row", "dp"), "col"),
            P(("row", "dp")),
            P("col"),
        ),
        check_vma=False,
    )
```

```python
import functools

import jax
import jax.numpy as jnp
from jax import lax
from jax.experimental import pallas as pl
from jax.experimental.pallas import tpu as pltpu
from jax.sharding import PartitionSpec as P


STEP = 10
F32 = jnp.float32
BF16 = jnp.bfloat16
OWN = 448
HALF = 512
SPAN = 512
LANES = 128
CORR_ONE = 1.0 - 0.9**STEP
CORR_TWO = 1.0 - 0.999**STEP
ANY = pl.BlockSpec(memory_space=pl.ANY)


SMALL = pltpu.CompilerParams(vmem_limit_bytes=16 << 20)
GRANT = pltpu.CompilerParams(vmem_limit_bytes=58 << 20)


def in_hbm(a):
    return pltpu.with_memory_space_constraint(a, pltpu.MemorySpace.HBM)


def dot(left, right):
    return lax.dot_general(left, right, (((0,), (0,)), ((), ())), preferred_element_type=F32)


STEPS = (2, 1, 3, 0)


def owner(p, q):
    dp, core = lax.axis_index("dp"), lax.axis_index("row")
    along_x, along_y = jnp.where(core == 0, p, q), jnp.where(core == 0, q, p)
    return 4 * (((dp >> 2) + along_y) & 3) + ((dp + along_x) & 3)


def product_kernel(p, halves, split, hidden, upstream, *refs):
    received, refs = refs[: -6 - split * len(halves)], refs[-6 - split * len(halves) :]
    outs, (held, features, got, made, total, sems) = refs[:-6], refs[-6:]
    width = HALF * len(halves)
    owners = [owner(p, q) for q in STEPS]
    loads = [
        pltpu.make_async_copy(
            hidden.at[:, pl.ds(pl.multiple_of(((7 * o) >> 1) * LANES, LANES), SPAN)],
            held.at[i],
            sems.at[i],
        )
        for i, o in enumerate(owners)
    ]
    feature_copy = pltpu.make_async_copy(
        upstream.at[:, pl.ds(halves[0] * HALF, width)], features, sems.at[4]
    )
    got_copies = [
        pltpu.make_async_copy(a, got.at[d], sems.at[5 + d]) for d, a in enumerate(received)
    ]
    feature_copy.start()
    for copy in loads:
        copy.start()
    for copy in got_copies:
        copy.start()
    feature_copy.wait()
    stores = []
    for i, o in enumerate(owners):
        loads[i].wait()
        total[i % 2] = dot(held[i], features[...])
        start = pl.multiple_of(64 * (o & 1), 64)
        if i == 0:
            for copy in got_copies:
                copy.wait()
        for d in range(len(halves)):
            value = total[i % 2, pl.ds(start, OWN), d * HALF : (d + 1) * HALF]
            if received:
                value = value + got[d, i].astype(F32)
            made[d, i] = value.astype(BF16)
            if split == 2:
                to = outs[0].at[i] if i < 3 else outs[1]
            else:
                to = outs[d].at[i]
            copy = pltpu.make_async_copy(made.at[d, i], to, sems.at[7 + 2 * i + d])
            copy.start()
            stores.append(copy)
    for copy in stores:
        copy.wait()


def product(hidden, upstream, p, halves=(0, 1), received=(), split=1):
    tokens = hidden.shape[0]
    count = len(halves)
    piece = jax.ShapeDtypeStruct((4, OWN, HALF), BF16)
    if split == 2:
        shapes = (
            jax.ShapeDtypeStruct((3, OWN, HALF), BF16),
            jax.ShapeDtypeStruct((OWN, HALF), BF16),
        )
    else:
        shapes = (piece,) * count
    return pl.pallas_call(
        functools.partial(product_kernel, p, halves, split),
        out_shape=shapes,
        in_specs=[ANY] * (2 + len(received)),
        out_specs=(ANY,) * len(shapes),
        scratch_shapes=[
            pltpu.VMEM((4, tokens, SPAN), BF16),
            pltpu.VMEM((tokens, HALF * count), BF16),
            pltpu.VMEM((count, 4, OWN, HALF) if received else (1, 1, 16, 128), BF16),
            pltpu.VMEM((count, 4, OWN, HALF), BF16),
            pltpu.VMEM((2, SPAN, HALF * count), F32),
            pltpu.SemaphoreType.DMA((15,)),
        ],
        cost_estimate=pl.CostEstimate(
            flops=8 * OWN * tokens * HALF * count, bytes_accessed=10 << 20, transcendentals=0
        ),
        compiler_params=GRANT,
    )(hidden, upstream, *received)


def ring(first_core, k):
    pairs = []
    for y in range(4):
        for x in range(4):
            for core in range(2):
                along_x = core == first_core
                to = 4 * y + (x + k) % 4 if along_x else 4 * ((y + k) % 4) + x
                pairs.append((2 * (4 * y + x) + core, 2 * to + core))
    return pairs


def near(k):
    return ring(0, k)


def other(k):
    return ring(1, k)


def send(value, pairs):
    return lax.ppermute(value, ("dp", "row"), pairs)


def sum_kernel(kept, got, far, up, down, held, made, sems):
    outs = (far, up, down)
    loads = [
        [
            pltpu.make_async_copy(a.at[k], held.at[k, n], sems.at[2 * k + n])
            for n, a in enumerate((kept, got))
        ]
        for k in range(3)
    ]
    for group in loads:
        for copy in group:
            copy.start()
    stores = []
    for k in range(3):
        for copy in loads[k]:
            copy.wait()
        made[k] = (held[k, 0].astype(F32) + held[k, 1].astype(F32)).astype(BF16)
        copy = pltpu.make_async_copy(made.at[k], outs[k], sems.at[6 + k])
        copy.start()
        stores.append(copy)
    for copy in stores:
        copy.wait()


def last(kept, got):
    message = jax.ShapeDtypeStruct((OWN, HALF), BF16)
    far, up, down = pl.pallas_call(
        sum_kernel,
        out_shape=(message,) * 3,
        in_specs=[ANY] * 2,
        out_specs=(ANY,) * 3,
        scratch_shapes=[
            pltpu.VMEM((3, 2, OWN, HALF), BF16),
            pltpu.VMEM((3, OWN, HALF), BF16),
            pltpu.SemaphoreType.DMA((9,)),
        ],
        cost_estimate=pl.CostEstimate(
            flops=3 * OWN * HALF, bytes_accessed=4 << 20, transcendentals=0
        ),
        compiler_params=SMALL,
    )(kept, got)
    return (send(far, other(2)), send(up, other(1)), send(down, other(-1)))


def reduced(hidden, upstream):
    far_low, far_high = product(hidden, upstream, 2)
    from_low = send(far_low, near(1))
    from_high = send(far_high, near(-1))
    (down_low,) = product(hidden, upstream, 3, (0,))
    direct_low = send(down_low, near(-1))
    (up_high,) = product(hidden, upstream, 1, (1,))
    direct_high = send(up_high, near(1))
    most, mine = product(hidden, upstream, 1, (0,), (from_low,), 2)
    added_low = send(most, near(1))
    added_low_own = send(mine, near(1))
    most, mine = product(hidden, upstream, 3, (1,), (from_high,), 2)
    added_high = send(most, near(-1))
    added_high_own = send(mine, near(-1))
    own_low, own_high = product(hidden, upstream, 0, (0, 1), (direct_low, direct_high))
    kept_low, kept_high = in_hbm(own_low), in_hbm(own_high)
    return (
        (own_low[3].astype(F32) + added_low_own.astype(F32), *last(kept_low, added_low)),
        (own_high[3].astype(F32) + added_high_own.astype(F32), *last(kept_high, added_high)),
    )


TALL = 224
CHUNKS = OWN // TALL


def second_kernel(half, own, far, up, down, codes, rows, columns, *refs):
    before, refs = (refs[:2], refs[2:]) if half else ((), refs)
    gradient, second, row_out, column_out, wide = refs
    i = pl.program_id(0)
    total = own[...]
    for ref in (far, up, down):
        total = total + ref[...].astype(F32)
    level = (codes[...].astype(F32) + 1.0) / 16.0
    old = jnp.minimum(rows[...], columns[...]) * level
    new = 0.999 * old + 0.001 * total * total
    gradient[...] = total
    second[...] = new
    peak = jnp.max(new, axis=0, keepdims=True)
    here = slice(half * HALF, (half + 1) * HALF)

    @pl.when(i == 0)
    def _():
        column_out[:, here] = peak
        if half:
            column_out[:, :HALF] = before[1][...]

    @pl.when(i > 0)
    def _():
        column_out[:, here] = jnp.maximum(column_out[:, here], peak)

    widest = new[:, :LANES]
    for b in range(1, HALF // LANES):
        widest = jnp.maximum(widest, new[:, b * LANES : (b + 1) * LANES])
    wide[pl.ds(pl.multiple_of(i * TALL, TALL), TALL), :] = widest

    @pl.when(i == pl.num_programs(0) - 1)
    def _():
        row_top = jnp.max(wide[...].T, axis=0, keepdims=True)
        row_out[...] = jnp.maximum(row_top, before[0][...]) if half else row_top


def second_moment(half, parts, codes, rows, columns, before=()):
    reach = HALF * (1 + half)
    half_spec = pl.BlockSpec((TALL, HALF), lambda i: (i, 0))

    def whole(width):
        return pl.BlockSpec((1, width), lambda i: (0, 0))

    return pl.pallas_call(
        functools.partial(second_kernel, half),
        out_shape=(
            jax.ShapeDtypeStruct((OWN, HALF), F32),
            jax.ShapeDtypeStruct((OWN, HALF), F32),
            jax.ShapeDtypeStruct((1, OWN), F32),
            jax.ShapeDtypeStruct((1, reach), F32),
        ),
        grid=(CHUNKS,),
        in_specs=[half_spec] * 4
        + [
            pl.BlockSpec((TALL, HALF), lambda i: (i, half)),
            pl.BlockSpec((TALL, 1), lambda i: (i, 0)),
            pl.BlockSpec((1, HALF), lambda i: (0, half)),
        ]
        + ([whole(OWN), whole(HALF)] if half else []),
        out_specs=(half_spec, half_spec, whole(OWN), whole(reach)),
        scratch_shapes=[pltpu.VMEM((OWN, LANES), F32)],
        cost_estimate=pl.CostEstimate(
            flops=20 * OWN * HALF, bytes_accessed=5 << 20, transcendentals=0
        ),
        compiler_params=SMALL,
    )(*parts, codes, rows, columns, *before)


def first_kernel(half, gradient, second, codes, scale, *refs):
    update, normed, peaks, tops = refs[-4:]
    blocks = HALF // LANES
    for b in range(blocks):
        here = slice(b * LANES, (b + 1) * LANES)
        block = half * blocks + b
        code = codes[:, here]
        upper = code >= 8
        expo = jnp.where(upper, code - 8, 7 - code)
        magnitude = jnp.where(expo > 0, lax.shift_left(jnp.ones_like(expo), expo), 0)
        table = jnp.where(upper, magnitude, -magnitude).astype(F32) * (1.0 / 128.0)
        new = 0.9 * (scale[:, block : block + 1] * table) + 0.1 * gradient[:, here]
        update[:, here] = new / CORR_ONE / (jnp.sqrt(second[:, here] / CORR_TWO) + 1e-08)
        peak = jnp.max(jnp.abs(new), axis=1, keepdims=True)
        normed[:, here] = (new / (peak + 1e-06)).astype(BF16)
        at = pl.ds(pl.multiple_of(pl.program_id(0) * TALL, TALL), TALL)
        tops[at, b : b + 1] = peak

    @pl.when(pl.program_id(0) == pl.num_programs(0) - 1)
    def _():
        mine = tops[...].T[:blocks]
        rest = refs[0][:blocks, :] if half else mine
        peaks[...] = jnp.concatenate([rest, mine] if half else [mine, rest], axis=0)


def first_moment(half, gradient, second, codes, scale, before=()):
    rows, width = codes.shape
    blocks = scale.shape[1]
    half_spec = pl.BlockSpec((TALL, HALF), lambda i: (i, 0))
    there_spec = pl.BlockSpec((TALL, HALF), lambda i: (i, half))
    scale_spec = pl.BlockSpec((TALL, blocks), lambda i: (i, 0))
    peak_spec = pl.BlockSpec((blocks, rows), lambda i: (0, 0))
    return pl.pallas_call(
        functools.partial(first_kernel, half),
        out_shape=(
            jax.ShapeDtypeStruct((rows, width), F32),
            jax.ShapeDtypeStruct((rows, width), BF16),
            jax.ShapeDtypeStruct((blocks, rows), F32),
        ),
        grid=(CHUNKS,),
        in_specs=[half_spec, half_spec, there_spec, scale_spec]
        + ([peak_spec, ANY, ANY] if half else []),
        out_specs=(there_spec, there_spec, peak_spec),
        scratch_shapes=[pltpu.VMEM((rows, LANES), F32)],
        input_output_aliases={5: 0, 6: 1} if half else {},
        cost_estimate=pl.CostEstimate(
            flops=40 * rows * HALF, bytes_accessed=5 << 20, transcendentals=rows * HALF
        ),
        compiler_params=SMALL,
    )(gradient, second, codes, scale, *before)


def norm_kernel(low, high, row_peak, column_peak, normed):
    rows = low.shape[0]
    row = jnp.broadcast_to(row_peak[...], (LANES, rows)).T
    for n, second in enumerate((low, high)):
        for b in range(HALF // LANES):
            here = slice(b * LANES, (b + 1) * LANES)
            there = slice(n * HALF + b * LANES, n * HALF + (b + 1) * LANES)
            peak = jnp.minimum(row, column_peak[:, there]) + 1e-06
            normed[:, there] = (second[:, here] / peak).astype(BF16)


def norm_second(low, high, row_peak, column_peak):
    return pl.pallas_call(
        norm_kernel,
        out_shape=jax.ShapeDtypeStruct((OWN, 2 * HALF), BF16),
        compiler_params=SMALL,
        name="norm",
    )(low, high, row_peak, column_peak)


def ring_max(value, axis, way):
    parts = []
    for k in (1, 2, 3):
        parts.append(lax.ppermute(value, axis, way(k)))
    for part in parts:
        value = jnp.maximum(value, part)
    return value


def per_device(
    hidden, upstream, first_codes, first_scale, second_codes, second_rows, second_columns
):
    low, high = reduced(hidden, upstream)
    rows, columns = second_rows[:, None], second_columns[None, :]
    gradient_low, second_low, row_low, column_low = second_moment(
        0, low, second_codes, rows, columns
    )
    done = first_moment(0, gradient_low, second_low, first_codes, first_scale)
    gradient_high, second_high, row_peak, column_peak = second_moment(
        1, high, second_codes, rows, columns, (row_low, column_low)
    )
    both = ("dp", "row")
    partner = lax.ppermute(column_peak, "row", [(0, 1), (1, 0)])
    for k in (1, 3):
        beside = lax.ppermute(row_peak, "col", [(z, z ^ k) for z in range(4)])
        row_peak = jnp.maximum(row_peak, beside)
    column_peak = ring_max(jnp.maximum(column_peak, partner), both, near)
    column_peak = ring_max(column_peak, both, other)
    update_step, first_normed, first_peak = first_moment(
        1, gradient_high, second_high, first_codes, first_scale, (done[2], done[0], done[1])
    )
    second_normed = norm_second(second_low, second_high, row_peak, column_peak)
    return (
        update_step,
        first_normed,
        first_peak.T,
        second_normed,
        row_peak.reshape(-1),
        column_peak.reshape(-1),
    )


def solution(mesh):
    placed = (
        P("dp", "row"),
        P("dp", "col"),
        P(("row", "dp"), "col"),
        P(("row", "dp"), "col"),
        P(("row", "dp"), "col"),
        P(("row", "dp")),
        P("col"),
    )
    return jax.shard_map(
        per_device,
        mesh=mesh,
        in_specs=placed,
        out_specs=(
            P(("row", "dp"), "col"),
            P(("row", "dp"), "col"),
            P(("row", "dp"), "col"),
            P(("row", "dp"), "col"),
            P(("row", "dp")),
            P("col"),
        ),
        check_vma=False,
    )
```
